32 devices in a mesh: parts: 2 (over y), seq: 4 (over z), chan: 2 (over x), rep: 2 (over core).
Axes of the slice: x: 2, y: 2, z: 4, core: 2. Of those that a mesh axis runs over, the one named last changes fastest.
Arguments:
- tokens: bfloat16 [4096, 4096], P(('parts', 'seq'), ('chan', 'rep')), parts along dimension 0, may hold values from -6 to 6
- w_query: bfloat16 [4096, 4096], P('seq', ('chan', 'rep')), may hold values from -0.09375 to 0.09375
- w_key: bfloat16 [4096, 4096], P('seq', ('chan', 'rep')), may hold values from -0.09375 to 0.09375
- w_value: bfloat16 [4096, 4096], P('seq', ('chan', 'rep')), may hold values from -0.09375 to 0.09375
- decay_rate: float32 [4096, 16], P(('chan', 'rep', 'seq')), may hold values from 4.8828125e-06 to 0.04, as said below
- residue: float32 [4096, 16], P(('chan', 'rep', 'seq')), may hold values from -1.5 to 1.5
- carried: float32 [8192, 16], P(('parts', 'chan', 'rep', 'seq')), parts along dimension 0, may hold values from -6 to 6
Outputs:
- gated_output: bfloat16 [4096, 4096], P(('parts', 'seq'), ('chan', 'rep')), parts along dimension 0
- new_state: float32 [8192, 16], P(('parts', 'chan', 'rep', 'seq')), parts along dimension 0
The draws below stay inside these ranges and needn't reach their ends.
There are 2 independent parts, one for each index of `parts`. The reference program is written for one: setup_inputs(seed, part) draws one part's arguments, and reference() takes and returns one part's arrays. A program takes and returns all parts, laid end to end along the dimension named above; an argument that names none is the same for every part. Nothing has to cross between parts.
Inputs may be any that keep to these rules, and one draw needn't show every extreme that they name: `decay_rate`: each rate lies between 0.01 / 2048 and 0.04.
All inputs are finite; a program needn't handle non-finite values.
Results may differ from the reference program's by a relative error of at most 0.0066.
Values may be sent and summed in bfloat16 or wider, within the bound.
A program may use at most 128 MiB of HBM per device.

```python
import math
import jax
import jax.numpy as jnp
from jax import lax

D = 4096
MODES = 16
LENGTH = 2048


def draw_decay_rate(key, part):
    lowest = 0.01 / LENGTH
    subkeys = jax.random.split(key, 1)
    return jnp.exp(jax.random.uniform(subkeys[0], (D, MODES), jnp.float32, math.log(lowest), math.log(0.04))).astype(jnp.float32)


def level_of(own_key, extent, cuts, least, top_value):
    def one(dim, parts):
        heights = jax.random.uniform(jax.random.fold_in(jax.random.fold_in(own_key, 6), dim), (parts,), jnp.float32, least / len(cuts), top_value / len(cuts))
        return jnp.repeat(jnp.exp(heights), extent[dim] // parts).reshape((-1,) + (1,) * (len(extent) - dim - 1))

    gain = one(*cuts[0])
    for cut in cuts[1:]:
        gain = gain * one(*cut)
    return gain


def noise(stream_key, extent, scale, bound, cuts=(), kind=jnp.bfloat16):
    loudness = level_of(stream_key, extent, cuts, -0.22, 0.18) if cuts else 1.0
    values = jax.random.normal(stream_key, extent, jnp.float32) * scale * loudness
    return jnp.minimum(jnp.maximum(values, -bound), bound).astype(kind)


def setup_inputs(seed: int = 0, part: int = 0) -> dict:
    key_of = jax.random.split(jax.random.key(seed), 8)
    part_keys = jax.random.split(jax.random.fold_in(key_of[7], part), 8)
    tokens = noise(part_keys[0], (LENGTH, D), 1.0, 6.0, ((0, 4), (1, 4)))
    w_query = noise(key_of[1], (D, D), D ** -0.5, 0.09375, ((0, 4), (1, 4)))
    w_key = noise(key_of[2], (D, D), D ** -0.5, 0.09375, ((0, 4), (1, 4)))
    w_value = noise(key_of[3], (D, D), D ** -0.5, 0.09375, ((0, 4), (1, 4)))
    decay_rate = draw_decay_rate(jax.random.fold_in(key_of[7], 71), part)
    residue = noise(key_of[5], (D, MODES), 0.25, 1.5, ((0, 16),), jnp.float32)
    carried = noise(part_keys[6], (D, MODES), 1.0, 6.0, ((0, 16),), jnp.float32)
    return {"tokens": tokens, "w_query": w_query, "w_key": w_key, "w_value": w_value, "decay_rate": decay_rate, "residue": residue, "carried": carried}


def channel_group(operands):
    signal, decay_rates, residues, start_state = operands
    seq_length = signal.shape[1]
    offsets = jnp.arange(seq_length, dtype=jnp.float32)
    scaling = jnp.sqrt(-jnp.expm1(-2.0 * decay_rates))
    powers = jnp.exp(-decay_rates[:, :, None] * offsets[None, None, :])
    kernel = lax.optimization_barrier(jnp.sum((residues * scaling)[:, :, None] * powers, axis=1))
    padded_size = 2 * seq_length
    spectrum = jnp.fft.rfft(signal, padded_size) * jnp.fft.rfft(kernel, padded_size)
    direct = jnp.fft.irfft(spectrum, padded_size)[:, :seq_length]
    carried_part = lax.optimization_barrier(jnp.sum((residues * start_state * jnp.exp(-decay_rates))[:, :, None] * powers, axis=1))
    final_state = jnp.exp(-decay_rates * seq_length) * start_state + scaling * lax.optimization_barrier(jnp.sum(powers[:, :, ::-1] * signal[:, None, :], axis=2))
    return (direct + carried_part, final_state)

def reference(tokens, w_query, w_key, w_value, decay_rate, residue, carried):
    query_rows = jnp.dot(tokens, w_query, preferred_element_type=jnp.float32).astype(jnp.bfloat16)
    key_rows = jnp.dot(tokens, w_key, preferred_element_type=jnp.float32).astype(jnp.bfloat16)
    value_rows = jnp.dot(tokens, w_value, preferred_element_type=jnp.float32).astype(jnp.bfloat16)
    query_rows, key_rows, value_rows = lax.optimization_barrier((query_rows, key_rows, value_rows))
    product = (key_rows.astype(jnp.float32) * value_rows.astype(jnp.float32)).astype(jnp.bfloat16)
    product = lax.optimization_barrier(product)
    signal = product.astype(jnp.float32).T
    groups = D // 256
    conv, final_state = lax.map(channel_group, (signal.reshape(groups, 256, -1), decay_rate.reshape(groups, 256, -1), residue.reshape(groups, 256, -1), carried.reshape(groups, 256, -1)))
    conv = conv.reshape(D, -1).astype(jnp.bfloat16)
    conv = lax.optimization_barrier(conv)
    gated_output = (query_rows.astype(jnp.float32) * conv.T.astype(jnp.float32)).astype(jnp.bfloat16)
    return (gated_output, final_state.reshape(D, -1))
```

```python
import functools

import jax
import jax.numpy as jnp
from jax import lax
from jax.experimental import pallas as pl
from jax.experimental.pallas import tpu as pltpu
from jax.sharding import PartitionSpec as P

BLOCK = 128
LANES = 128
CHUNKS = 8


HIGHEST_PRECISION = lax.Precision.HIGHEST


def mode_scale(decay_rates):
    return jnp.sqrt(-jnp.expm1(-2.0 * decay_rates))


def local_ends(blocks, decay_rates):
    block_width = blocks.shape[2]
    offsets = jnp.arange(block_width, dtype=jnp.float32)
    tail_powers = jnp.exp(-decay_rates[:, :, None] * (block_width - 1.0 - offsets)[None, None, :])
    sums_here = jnp.einsum("cnb,cmb->cnm", blocks, tail_powers, precision=HIGHEST_PRECISION)
    return mode_scale(decay_rates)[:, None, :] * sums_here


def combine_states(earlier, later):
    return (earlier[0] * later[0], later[0] * earlier[1] + later[1])


def block_sums(block_ends, decay_rates, block_width):
    step_decay = jnp.broadcast_to(jnp.exp(-decay_rates * block_width)[:, None, :], block_ends.shape)
    unused_decay, running = lax.associative_scan(combine_states, (step_decay, block_ends), axis=1)
    return running


def entering_states(running, decay_rates, start_state, block_width):
    count_blocks = running.shape[1]
    block_starts = jnp.arange(count_blocks, dtype=jnp.float32) * block_width
    decayed = (
        jnp.exp(-decay_rates[:, None, :] * block_starts[None, :, None]) * start_state[:, None, :]
    )
    earlier_sums = jnp.concatenate([jnp.zeros_like(running[:, :1]), running[:, :-1]], axis=1)
    final_state = (
        jnp.exp(-decay_rates * (count_blocks * block_width)) * start_state + running[:, -1]
    )
    return (decayed + earlier_sums, final_state)


def block_convolve(blocks, decay_rates, residues, entering):
    block_width = blocks.shape[2]
    offsets = jnp.arange(block_width, dtype=jnp.float32)
    powers = jnp.exp(-decay_rates[:, :, None] * offsets[None, None, :])
    kernel = jnp.sum((residues * mode_scale(decay_rates))[:, :, None] * powers, axis=1)
    out_index = jnp.arange(block_width, dtype=jnp.int32)[:, None]
    in_index = jnp.arange(block_width, dtype=jnp.int32)[None, :]
    lag = jnp.maximum(out_index - in_index, 0)
    causal = (out_index >= in_index).astype(jnp.float32)
    toeplitz = kernel[:, lag] * causal[None, :, :]
    direct = jnp.einsum("cij,cnj->cni", toeplitz, blocks, precision=HIGHEST_PRECISION)
    leading = residues[:, :, None] * jnp.exp(
        -decay_rates[:, :, None] * (offsets + 1.0)[None, None, :]
    )
    return direct + jnp.einsum("cnm,cmb->cnb", entering, leading, precision=HIGHEST_PRECISION)


def per_device(tokens, w_query, w_key, w_value, decay_rate, residue, carried):
    gathered = lax.all_gather(tokens, ("chan", "rep"), axis=1, tiled=True)
    pieces = (
        lax.all_gather(w_query, "seq", axis=0, tiled=True),
        lax.all_gather(w_key, "seq", axis=0, tiled=True),
        lax.all_gather(w_value, "seq", axis=0, tiled=True),
    )
    query_acc, key_acc, value_acc = tuple(
        (
            lax.dot_general(
                weight_piece, gathered, (((0,), (1,)), ((), ())), preferred_element_type=jnp.float32
            )
            for weight_piece in pieces
        )
    )
    query_rows = query_acc.astype(jnp.bfloat16)
    key_rows = key_acc.astype(jnp.bfloat16)
    value_rows = value_acc.astype(jnp.bfloat16)
    query_rows, key_rows, value_rows = lax.optimization_barrier((query_rows, key_rows, value_rows))
    product = (key_rows.astype(jnp.float32) * value_rows.astype(jnp.float32)).astype(jnp.bfloat16)
    owned = lax.all_to_all(product, "seq", split_axis=0, concat_axis=1, tiled=True)
    own_chan = owned.shape[0]
    blocks = owned.astype(jnp.float32).reshape(own_chan, -1, BLOCK)
    block_end = local_ends(blocks, decay_rate)
    running = block_sums(block_end, decay_rate, BLOCK)
    entering, new_state = entering_states(running, decay_rate, carried, BLOCK)
    conv_out = (
        block_convolve(blocks, decay_rate, residue, entering)
        .reshape(own_chan, -1)
        .astype(jnp.bfloat16)
    )
    conv_back = lax.all_to_all(conv_out, "seq", split_axis=1, concat_axis=0, tiled=True)
    conv_back = lax.optimization_barrier(conv_back)
    gated_rows = (query_rows.astype(jnp.float32) * conv_back.astype(jnp.float32)).astype(
        jnp.bfloat16
    )
    return (gated_rows.T, new_state)


def scan_kernel(q_ref, k_ref, v_ref, rate_ref, scale_ref, residue_ref, carried_ref, gated_ref,
                state_ref, signal, ends, entering, conv):
    length, width = q_ref.shape
    modes = rate_ref.shape[0]
    chunk = length // CHUNKS
    rows_at = 256
    for lane in range(0, width, LANES):
        lanes = pl.ds(lane, LANES)

        def multiply(step, _):
            rows = pl.ds(pl.multiple_of(step * rows_at, rows_at), rows_at)
            product = k_ref[rows, lanes].astype(jnp.float32) * v_ref[rows, lanes].astype(jnp.float32)
            signal[rows, :] = product.astype(jnp.bfloat16).astype(jnp.float32)
            return 0

        lax.fori_loop(0, length // rows_at, multiply, 0)
        rates = rate_ref[:, lanes]
        residues = residue_ref[:, lanes]
        scale = scale_ref[:, lanes]
        decay = jnp.exp(-rates)
        weight = residues * scale
        chunk_decay = jnp.exp(-rates * chunk)

        def rows_of(array):
            return [jnp.broadcast_to(array[m : m + 1, :], (CHUNKS, LANES)) for m in range(modes)]

        decays = rows_of(decay)
        weights = rows_of(weight)

        def sums(step, states):
            here = signal[pl.ds(step, CHUNKS, stride=chunk), :]
            return tuple(d * s + here for d, s in zip(decays, states))

        zero = jnp.zeros((CHUNKS, LANES), jnp.float32)
        finals = lax.fori_loop(0, chunk, sums, (zero,) * modes, unroll=4)
        for m in range(modes):
            ends[m] = finals[m]
        state = carried_ref[:, lanes]
        for c in range(CHUNKS):
            entering[:, c, :] = residues * state
            state = chunk_decay * state + scale * ends[:, c, :]
        state_ref[:, lanes] = state

        def outputs(step, states):
            here = signal[pl.ds(step, CHUNKS, stride=chunk), :]
            states = tuple(d * s + w * here for d, s, w in zip(decays, states, weights))
            terms = list(states)
            while len(terms) > 1:
                terms = [a + b for a, b in zip(terms[::2], terms[1::2])] + (
                    [terms[-1]] if len(terms) % 2 else []
                )
            conv[pl.ds(step, CHUNKS, stride=chunk), :] = terms[0]
            return states

        starts = tuple(entering[m] for m in range(modes))
        lax.fori_loop(0, chunk, outputs, starts, unroll=4)

        def gate(step, _):
            rows = pl.ds(pl.multiple_of(step * rows_at, rows_at), rows_at)
            rounded = conv[rows, :].astype(jnp.bfloat16).astype(jnp.float32)
            gated_ref[rows, lanes] = (q_ref[rows, lanes].astype(jnp.float32) * rounded).astype(
                jnp.bfloat16
            )
            return 0

        lax.fori_loop(0, length // rows_at, gate, 0)


def gated_scan(rows, rate, residue, carried):
    length = rows.shape[0]
    width, modes = rate.shape
    vmem = pl.BlockSpec(memory_space=pltpu.VMEM)
    gated, state = pl.pallas_call(
        scan_kernel,
        grid=(1,),
        out_shape=(
            jax.ShapeDtypeStruct((length, width), jnp.bfloat16),
            jax.ShapeDtypeStruct((modes, width), jnp.float32),
        ),
        in_specs=[pl.BlockSpec((length, width), functools.partial(lambda j, i: (0, j), j)) for j in range(3)]
        + [vmem] * 4,
        out_specs=(pl.BlockSpec((length, width), lambda i: (0, 0)), vmem),
        scratch_shapes=[
            pltpu.VMEM((length, LANES), jnp.float32),
            pltpu.VMEM((modes, CHUNKS, LANES), jnp.float32),
            pltpu.VMEM((modes, CHUNKS, LANES), jnp.float32),
            pltpu.VMEM((length, LANES), jnp.float32),
        ],
        compiler_params=pltpu.CompilerParams(vmem_limit_bytes=32 * 2**20),
    )(rows, rows, rows, rate.T, mode_scale(rate).T, residue.T, carried.T)
    return gated, state.T


def per_device_channels(tokens, w_query, w_key, w_value, decay_rate, residue, carried):
    gathered = lax.all_gather(tokens, ("chan", "rep"), axis=1, tiled=True)
    gathered = lax.all_gather(gathered, "seq", axis=0, tiled=True)
    weights = jnp.concatenate(
        [
            lax.all_to_all(w, "seq", split_axis=1, concat_axis=0, tiled=True)
            for w in (w_query, w_key, w_value)
        ],
        axis=1,
    )
    rows = lax.dot_general(
        gathered, weights, (((1,), (0,)), ((), ())), preferred_element_type=jnp.float32
    ).astype(jnp.bfloat16)
    gated, new_state = gated_scan(rows, decay_rate, residue, carried)
    gated = lax.all_to_all(gated, "seq", split_axis=0, concat_axis=1, tiled=True)
    return gated, new_state


def solution(mesh):
    in_specs = (
        P(("parts", "seq"), ("chan", "rep")),
        P("seq", ("chan", "rep")),
        P("seq", ("chan", "rep")),
        P("seq", ("chan", "rep")),
        P(("chan", "rep", "seq"), None),
        P(("chan", "rep", "seq"), None),
        P(("parts", "chan", "rep", "seq"), None),
    )
    out_specs = (P(("parts", "seq"), ("chan", "rep")), P(("parts", "chan", "rep", "seq"), None))

    def body(*arrays):
        own_channels = arrays[4].shape[0]
        chosen = per_device_channels if own_channels % LANES == 0 else per_device
        return chosen(*arrays)

    return jax.shard_map(body, mesh=mesh, in_specs=in_specs, out_specs=out_specs, check_vma=False)
```

```python
import functools

import jax
import jax.numpy as jnp
from jax import lax
from jax.experimental import pallas as pl
from jax.experimental.pallas import tpu as pltpu
from jax.sharding import PartitionSpec as P

BLOCK = 128
LANES = 128
CHUNKS = 8


HIGHEST_PRECISION = lax.Precision.HIGHEST


def mode_scale(decay_rates):
    return jnp.sqrt(-jnp.expm1(-2.0 * decay_rates))


def local_ends(blocks, decay_rates):
    block_width = blocks.shape[2]
    offsets = jnp.arange(block_width, dtype=jnp.float32)
    tail_powers = jnp.exp(-decay_rates[:, :, None] * (block_width - 1.0 - offsets)[None, None, :])
    sums_here = jnp.einsum("cnb,cmb->cnm", blocks, tail_powers, precision=HIGHEST_PRECISION)
    return mode_scale(decay_rates)[:, None, :] * sums_here


def combine_states(earlier, later):
    return (earlier[0] * later[0], later[0] * earlier[1] + later[1])


def block_sums(block_ends, decay_rates, block_width):
    step_decay = jnp.broadcast_to(jnp.exp(-decay_rates * block_width)[:, None, :], block_ends.shape)
    unused_decay, running = lax.associative_scan(combine_states, (step_decay, block_ends), axis=1)
    return running


def entering_states(running, decay_rates, start_state, block_width):
    count_blocks = running.shape[1]
    block_starts = jnp.arange(count_blocks, dtype=jnp.float32) * block_width
    decayed = (
        jnp.exp(-decay_rates[:, None, :] * block_starts[None, :, None]) * start_state[:, None, :]
    )
    earlier_sums = jnp.concatenate([jnp.zeros_like(running[:, :1]), running[:, :-1]], axis=1)
    final_state = (
        jnp.exp(-decay_rates * (count_blocks * block_width)) * start_state + running[:, -1]
    )
    return (decayed + earlier_sums, final_state)


def block_convolve(blocks, decay_rates, residues, entering):
    block_width = blocks.shape[2]
    offsets = jnp.arange(block_width, dtype=jnp.float32)
    powers = jnp.exp(-decay_rates[:, :, None] * offsets[None, None, :])
    kernel = jnp.sum((residues * mode_scale(decay_rates))[:, :, None] * powers, axis=1)
    out_index = jnp.arange(block_width, dtype=jnp.int32)[:, None]
    in_index = jnp.arange(block_width, dtype=jnp.int32)[None, :]
    lag = jnp.maximum(out_index - in_index, 0)
    causal = (out_index >= in_index).astype(jnp.float32)
    toeplitz = kernel[:, lag] * causal[None, :, :]
    direct = jnp.einsum("cij,cnj->cni", toeplitz, blocks, precision=HIGHEST_PRECISION)
    leading = residues[:, :, None] * jnp.exp(
        -decay_rates[:, :, None] * (offsets + 1.0)[None, None, :]
    )
    return direct + jnp.einsum("cnm,cmb->cnb", entering, leading, precision=HIGHEST_PRECISION)


def per_device(tokens, w_query, w_key, w_value, decay_rate, residue, carried):
    gathered = lax.all_gather(tokens, ("chan", "rep"), axis=1, tiled=True)
    pieces = (
        lax.all_gather(w_query, "seq", axis=0, tiled=True),
        lax.all_gather(w_key, "seq", axis=0, tiled=True),
        lax.all_gather(w_value, "seq", axis=0, tiled=True),
    )
    query_acc, key_acc, value_acc = tuple(
        (
            lax.dot_general(
                weight_piece, gathered, (((0,), (1,)), ((), ())), preferred_element_type=jnp.float32
            )
            for weight_piece in pieces
        )
    )
    query_rows = query_acc.astype(jnp.bfloat16)
    key_rows = key_acc.astype(jnp.bfloat16)
    value_rows = value_acc.astype(jnp.bfloat16)
    query_rows, key_rows, value_rows = lax.optimization_barrier((query_rows, key_rows, value_rows))
    product = (key_rows.astype(jnp.float32) * value_rows.astype(jnp.float32)).astype(jnp.bfloat16)
    owned = lax.all_to_all(product, "seq", split_axis=0, concat_axis=1, tiled=True)
    own_chan = owned.shape[0]
    blocks = owned.astype(jnp.float32).reshape(own_chan, -1, BLOCK)
    block_end = local_ends(blocks, decay_rate)
    running = block_sums(block_end, decay_rate, BLOCK)
    entering, new_state = entering_states(running, decay_rate, carried, BLOCK)
    conv_out = (
        block_convolve(blocks, decay_rate, residue, entering)
        .reshape(own_chan, -1)
        .astype(jnp.bfloat16)
    )
    conv_back = lax.all_to_all(conv_out, "seq", split_axis=1, concat_axis=0, tiled=True)
    conv_back = lax.optimization_barrier(conv_back)
    gated_rows = (query_rows.astype(jnp.float32) * conv_back.astype(jnp.float32)).astype(
        jnp.bfloat16
    )
    return (gated_rows.T, new_state)


def scan_kernel(q_ref, k_ref, v_ref, rate_ref, scale_ref, residue_ref, carried_ref, gated_ref,
                state_ref, signal, ends, entering, conv):
    length, width = q_ref.shape
    modes = rate_ref.shape[0]
    chunk = length // CHUNKS
    rows_at = 256
    for lane in range(0, width, LANES):
        lanes = pl.ds(lane, LANES)

        def multiply(step, _):
            rows = pl.ds(pl.multiple_of(step * rows_at, rows_at), rows_at)
            product = k_ref[rows, lanes].astype(jnp.float32) * v_ref[rows, lanes].astype(jnp.float32)
            signal[rows, :] = product.astype(jnp.bfloat16).astype(jnp.float32)
            return 0

        lax.fori_loop(0, length // rows_at, multiply, 0)
        rates = rate_ref[:, lanes]
        residues = residue_ref[:, lanes]
        scale = scale_ref[:, lanes]
        decay = jnp.exp(-rates)
        weight = residues * scale
        chunk_decay = jnp.exp(-rates * chunk)

        def rows_of(array):
            return [jnp.broadcast_to(array[m : m + 1, :], (CHUNKS, LANES)) for m in range(modes)]

        decays = rows_of(decay)
        weights = rows_of(weight)

        def sums(step, states):
            here = signal[pl.ds(step, CHUNKS, stride=chunk), :]
            return tuple(d * s + here for d, s in zip(decays, states))

        zero = jnp.zeros((CHUNKS, LANES), jnp.float32)
        finals = lax.fori_loop(0, chunk, sums, (zero,) * modes, unroll=4)
        for m in range(modes):
            ends[m] = finals[m]
        state = carried_ref[:, lanes]
        for c in range(CHUNKS):
            entering[:, c, :] = residues * state
            state = chunk_decay * state + scale * ends[:, c, :]
        state_ref[:, lanes] = state

        def outputs(step, states):
            here = signal[pl.ds(step, CHUNKS, stride=chunk), :]
            states = tuple(d * s + w * here for d, s, w in zip(decays, states, weights))
            terms = list(states)
            while len(terms) > 1:
                terms = [a + b for a, b in zip(terms[::2], terms[1::2])] + (
                    [terms[-1]] if len(terms) % 2 else []
                )
            conv[pl.ds(step, CHUNKS, stride=chunk), :] = terms[0]
            return states

        starts = tuple(entering[m] for m in range(modes))
        lax.fori_loop(0, chunk, outputs, starts, unroll=4)

        def gate(step, _):
            rows = pl.ds(pl.multiple_of(step * rows_at, rows_at), rows_at)
            rounded = conv[rows, :].astype(jnp.bfloat16).astype(jnp.float32)
            gated_ref[rows, lanes] = (q_ref[rows, lanes].astype(jnp.float32) * rounded).astype(
                jnp.bfloat16
            )
            return 0

        lax.fori_loop(0, length // rows_at, gate, 0)


def gated_scan(rows, rate, residue, carried):
    length = rows.shape[0]
    width, modes = rate.shape
    vmem = pl.BlockSpec(memory_space=pltpu.VMEM)
    gated, state = pl.pallas_call(
        scan_kernel,
        grid=(1,),
        out_shape=(
            jax.ShapeDtypeStruct((length, width), jnp.bfloat16),
            jax.ShapeDtypeStruct((modes, width), jnp.float32),
        ),
        in_specs=[pl.BlockSpec((length, width), functools.partial(lambda j, i: (0, j), j)) for j in range(3)]
        + [vmem] * 4,
        out_specs=(pl.BlockSpec((length, width), lambda i: (0, 0)), vmem),
        scratch_shapes=[
            pltpu.VMEM((length, LANES), jnp.float32),
            pltpu.VMEM((modes, CHUNKS, LANES), jnp.float32),
            pltpu.VMEM((modes, CHUNKS, LANES), jnp.float32),
            pltpu.VMEM((length, LANES), jnp.float32),
        ],
        compiler_params=pltpu.CompilerParams(vmem_limit_bytes=32 * 2**20),
    )(rows, rows, rows, rate.T, mode_scale(rate).T, residue.T, carried.T)
    return gated, state.T


MESH = pl.DeviceIdType.MESH
PIECES = 2


def gather_kernel(count, tokens_ref, query_ref, key_ref, value_ref, all_ref, weights_ref,
                  tokens_vmem, weights_vmem, local_sem, fill_sem,
                  hop_send, hop_recv, side_send, side_recv, core_send, core_recv,
                  part_send, part_recv, layer_send, layer_recv):
    part, seq, chan, rep = (lax.axis_index(a) for a in ("parts", "seq", "chan", "rep"))
    rows, columns = tokens_ref.shape
    depth, outer = query_ref.shape
    width = outer // count
    half = depth // 2
    piece = rows // PIECES
    matrices = (query_ref, key_ref, value_ref)

    barrier = pltpu.get_barrier_semaphore()
    mates = ({"parts": 1 - part}, {"chan": 1 - chan}, {"rep": 1 - rep})
    for mate in mates:
        pl.semaphore_signal(barrier, inc=1, device_id=mate, device_id_type=MESH)
    for step in range(1, count):
        pl.semaphore_signal(
            barrier, inc=1, device_id={"seq": lax.rem(seq + step, count)}, device_id_type=MESH
        )
    pl.semaphore_wait(barrier, count - 1 + len(mates))

    def token_block(block, side, core, p):
        top = pl.multiple_of(block * rows + p * piece, piece)
        left = pl.multiple_of((side * 2 + core) * columns, columns)
        return all_ref.at[pl.ds(top, piece), pl.ds(left, columns)]

    def own_piece(p):
        return tokens_ref.at[pl.ds(p * piece, piece), :]

    def remote(source, target, send, recv, device):
        return pltpu.make_async_remote_copy(
            src_ref=source, dst_ref=target, send_sem=send, recv_sem=recv,
            device_id=device, device_id_type=MESH,
        )

    def hop(block, p, way, source=None):
        here = token_block(block, chan, rep, p)
        device = {"seq": seq + 1 if way == 0 else seq - 1}
        return remote(here if source is None else source, here, hop_send.at[block, p, way], hop_recv.at[block, p], device)

    def side(block, p, source=None):
        here = token_block(block, chan, rep, p)
        return remote(here if source is None else source, here, side_send.at[block, p], side_recv.at[block, p], {"chan": 1 - chan})

    def side_arrival(block, p):
        there = token_block(block, 1 - chan, rep, p)
        return remote(there, there, side_send.at[block, p], side_recv.at[block, p], {"chan": 1 - chan})

    def core(block, which, p, source=None):
        here = token_block(block, chan if which == 0 else 1 - chan, rep, p)
        return remote(here if source is None else source, here, core_send.at[block, which, p], core_recv.at[block, which, p], {"rep": 1 - rep})

    def core_arrival(block, which, p):
        there = token_block(block, chan if which == 0 else 1 - chan, 1 - rep, p)
        return remote(there, there, core_send.at[block, which, p], core_recv.at[block, which, p], {"rep": 1 - rep})

    def weight_block(block, m, part_of):
        top = pl.multiple_of(block * depth + part_of * half, half)
        return weights_ref.at[pl.ds(top, half), pl.ds(m * width, width)]

    def spread(target, m):
        source = matrices[m].at[
            pl.ds(pl.multiple_of(part * half, half), half),
            pl.ds(pl.multiple_of(target * width, width), width),
        ]
        return remote(source, weight_block(seq, m, part), layer_send.at[target, m], layer_recv.at[seq, m], {"seq": target})

    def spread_arrival(block, m):
        here = weight_block(block, m, part)
        return remote(here, here, layer_send.at[block, m], layer_recv.at[block, m], {"seq": block})

    def swap(block, m):
        here = weight_block(block, m, part)
        return remote(here, here, part_send.at[block, m], part_recv.at[block, m], {"parts": 1 - part})

    def swap_arrival(block, m):
        there = weight_block(block, m, 1 - part)
        return remote(there, there, part_send.at[block, m], part_recv.at[block, m], {"parts": 1 - part})

    def sources(distance):
        return ((seq >= distance, seq - distance, 0), (seq + distance < count, seq + distance, 1))

    def has_next(way):
        return seq + 1 < count if way == 0 else seq >= 1

    def send_weights(distance):
        for there, other, _ in sources(distance):
            @pl.when(there)
            def _():
                for m in range(3):
                    spread(other, m).start()

    fills = [pltpu.make_async_copy(tokens_ref, tokens_vmem, fill_sem.at[3])] + [
        pltpu.make_async_copy(
            matrices[m].at[:, pl.ds(pl.multiple_of(seq * width, width), width)],
            weights_vmem.at[:, pl.ds(m * width, width)], fill_sem.at[m])
        for m in range(3)
    ]
    for p in range(PIECES):
        for way in range(2):
            @pl.when(has_next(way))
            def _():
                hop(seq, p, way, own_piece(p)).start()
        side(seq, p, own_piece(p)).start()
        core(seq, 0, p, own_piece(p)).start()
    send_weights(1)
    for fill in fills:
        fill.start()
    for fill in fills:
        fill.wait()
    locals_ = [
        pltpu.make_async_copy(
            tokens_vmem,
            all_ref.at[pl.ds(pl.multiple_of(seq * rows, rows), rows),
                       pl.ds(pl.multiple_of((chan * 2 + rep) * columns, columns), columns)],
            local_sem.at[0]),
        pltpu.make_async_copy(
            weights_vmem, weights_ref.at[pl.ds(pl.multiple_of(seq * depth, depth), depth), :],
            local_sem.at[1]),
    ]
    for copy in locals_:
        copy.start()

    def pass_side(block):
        for p in range(PIECES):
            side_arrival(block, p).wait_recv()
            core(block, 1, p).start()

    for distance in range(1, count):
        for p in range(PIECES):
            for there, other, way in sources(distance):
                @pl.when(there)
                def _():
                    hop(other, p, way).wait_recv()

                    @pl.when(has_next(way))
                    def _():
                        hop(other, p, way).start()

                    side(other, p).start()
                    core(other, 0, p).start()
        if distance + 1 < count:
            send_weights(distance + 1)
        for m in range(3):
            for there, other, _ in sources(distance):
                @pl.when(there)
                def _():
                    spread_arrival(other, m).wait_recv()
                    swap(other, m).start()
        if distance == 1:
            pass_side(seq)
        else:
            for there, other, _ in sources(distance - 1):
                @pl.when(there)
                def _():
                    pass_side(other)
    for there, other, _ in sources(count - 1):
        @pl.when(there)
        def _():
            pass_side(other)

    for copy in locals_:
        copy.wait()
    for p in range(PIECES):
        for way in range(2):
            @pl.when(has_next(way))
            def _():
                hop(seq, p, way, own_piece(p)).wait_send()
        side(seq, p, own_piece(p)).wait_send()
        core(seq, 0, p, own_piece(p)).wait_send()
        core(seq, 1, p).wait_send()
        for which in range(2):
            core_arrival(seq, which, p).wait_recv()
    for distance in range(1, count):
        for there, other, way in sources(distance):
            @pl.when(there)
            def _():
                for p in range(PIECES):
                    @pl.when(has_next(way))
                    def _():
                        hop(other, p, way).wait_send()

                    side(other, p).wait_send()
                    for which in range(2):
                        core(other, which, p).wait_send()
                        core_arrival(other, which, p).wait_recv()
                for m in range(3):
                    spread(other, m).wait_send()
                    swap(other, m).wait_send()
                    swap_arrival(other, m).wait_recv()


def gather(tokens, w_query, w_key, w_value, count):
    rows, columns = tokens.shape
    depth, outer = w_query.shape
    width = outer // count
    anywhere = pl.BlockSpec(memory_space=pl.ANY)
    dma = pltpu.SemaphoreType.DMA
    return pl.pallas_call(
        functools.partial(gather_kernel, count),
        out_shape=(
            jax.ShapeDtypeStruct((rows * count, columns * 4), jnp.bfloat16),
            jax.ShapeDtypeStruct((depth * count, width * 3), jnp.bfloat16),
        ),
        in_specs=[anywhere] * 4,
        out_specs=(anywhere, anywhere),
        scratch_shapes=[
            pltpu.VMEM((rows, columns), jnp.bfloat16),
            pltpu.VMEM((depth, width * 3), jnp.bfloat16),
            dma((2,)), dma((4,)),
            dma((count, PIECES, 2)), dma((count, PIECES)),
            dma((count, PIECES)), dma((count, PIECES)),
            dma((count, 2, PIECES)), dma((count, 2, PIECES)),
            dma((count, 3)), dma((count, 3)),
            dma((count, 3)), dma((count, 3)),
        ],
        compiler_params=pltpu.CompilerParams(collective_id=0, has_side_effects=True),
    )(tokens, w_query, w_key, w_value)


def per_device_channels(tokens, w_query, w_key, w_value, decay_rate, residue, carried):
    count = lax.axis_size("seq")
    gathered, weights = gather(tokens, w_query, w_key, w_value, count)
    rows = lax.dot_general(
        gathered, weights, (((1,), (0,)), ((), ())), preferred_element_type=jnp.float32
    ).astype(jnp.bfloat16)
    gated, new_state = gated_scan(rows, decay_rate, residue, carried)
    gated = lax.all_to_all(gated, "seq", split_axis=0, concat_axis=1, tiled=True)
    return gated, new_state


def solution(mesh):
    in_specs = (
        P(("parts", "seq"), ("chan", "rep")),
        P("seq", ("chan", "rep")),
        P("seq", ("chan", "rep")),
        P("seq", ("chan", "rep")),
        P(("chan", "rep", "seq"), None),
        P(("chan", "rep", "seq"), None),
        P(("parts", "chan", "rep", "seq"), None),
    )
    out_specs = (P(("parts", "seq"), ("chan", "rep")), P(("parts", "chan", "rep", "seq"), None))

    def body(*arrays):
        own_channels = arrays[4].shape[0]
        mates = all(mesh.shape[a] == 2 for a in ("parts", "chan", "rep"))
        chosen = per_device_channels if own_channels % LANES == 0 and mates else per_device
        return chosen(*arrays)

    return jax.shard_map(body, mesh=mesh, in_specs=in_specs, out_specs=out_specs, check_vma=False)
```

```python
import functools

import jax
import jax.numpy as jnp
from jax import lax
from jax.experimental import pallas as pl
from jax.experimental.pallas import tpu as pltpu
from jax.sharding import PartitionSpec as P

BLOCK = 128
LANES = 128
CHUNKS = 8


HIGHEST_PRECISION = lax.Precision.HIGHEST


def mode_scale(decay_rates):
    return jnp.sqrt(-jnp.expm1(-2.0 * decay_rates))


def local_ends(blocks, decay_rates):
    block_width = blocks.shape[2]
    offsets = jnp.arange(block_width, dtype=jnp.float32)
    tail_powers = jnp.exp(-decay_rates[:, :, None] * (block_width - 1.0 - offsets)[None, None, :])
    sums_here = jnp.einsum("cnb,cmb->cnm", blocks, tail_powers, precision=HIGHEST_PRECISION)
    return mode_scale(decay_rates)[:, None, :] * sums_here


def combine_states(earlier, later):
    return (earlier[0] * later[0], later[0] * earlier[1] + later[1])


def block_sums(block_ends, decay_rates, block_width):
    step_decay = jnp.broadcast_to(jnp.exp(-decay_rates * block_width)[:, None, :], block_ends.shape)
    unused_decay, running = lax.associative_scan(combine_states, (step_decay, block_ends), axis=1)
    return running


def entering_states(running, decay_rates, start_state, block_width):
    count_blocks = running.shape[1]
    block_starts = jnp.arange(count_blocks, dtype=jnp.float32) * block_width
    decayed = (
        jnp.exp(-decay_rates[:, None, :] * block_starts[None, :, None]) * start_state[:, None, :]
    )
    earlier_sums = jnp.concatenate([jnp.zeros_like(running[:, :1]), running[:, :-1]], axis=1)
    final_state = (
        jnp.exp(-decay_rates * (count_blocks * block_width)) * start_state + running[:, -1]
    )
    return (decayed + earlier_sums, final_state)


def block_convolve(blocks, decay_rates, residues, entering):
    block_width = blocks.shape[2]
    offsets = jnp.arange(block_width, dtype=jnp.float32)
    powers = jnp.exp(-decay_rates[:, :, None] * offsets[None, None, :])
    kernel = jnp.sum((residues * mode_scale(decay_rates))[:, :, None] * powers, axis=1)
    out_index = jnp.arange(block_width, dtype=jnp.int32)[:, None]
    in_index = jnp.arange(block_width, dtype=jnp.int32)[None, :]
    lag = jnp.maximum(out_index - in_index, 0)
    causal = (out_index >= in_index).astype(jnp.float32)
    toeplitz = kernel[:, lag] * causal[None, :, :]
    direct = jnp.einsum("cij,cnj->cni", toeplitz, blocks, precision=HIGHEST_PRECISION)
    leading = residues[:, :, None] * jnp.exp(
        -decay_rates[:, :, None] * (offsets + 1.0)[None, None, :]
    )
    return direct + jnp.einsum("cnm,cmb->cnb", entering, leading, precision=HIGHEST_PRECISION)


def per_device(tokens, w_query, w_key, w_value, decay_rate, residue, carried):
    gathered = lax.all_gather(tokens, ("chan", "rep"), axis=1, tiled=True)
    pieces = (
        lax.all_gather(w_query, "seq", axis=0, tiled=True),
        lax.all_gather(w_key, "seq", axis=0, tiled=True),
        lax.all_gather(w_value, "seq", axis=0, tiled=True),
    )
    query_acc, key_acc, value_acc = tuple(
        (
            lax.dot_general(
                weight_piece, gathered, (((0,), (1,)), ((), ())), preferred_element_type=jnp.float32
            )
            for weight_piece in pieces
        )
    )
    query_rows = query_acc.astype(jnp.bfloat16)
    key_rows = key_acc.astype(jnp.bfloat16)
    value_rows = value_acc.astype(jnp.bfloat16)
    query_rows, key_rows, value_rows = lax.optimization_barrier((query_rows, key_rows, value_rows))
    product = (key_rows.astype(jnp.float32) * value_rows.astype(jnp.float32)).astype(jnp.bfloat16)
    owned = lax.all_to_all(product, "seq", split_axis=0, concat_axis=1, tiled=True)
    own_chan = owned.shape[0]
    blocks = owned.astype(jnp.float32).reshape(own_chan, -1, BLOCK)
    block_end = local_ends(blocks, decay_rate)
    running = block_sums(block_end, decay_rate, BLOCK)
    entering, new_state = entering_states(running, decay_rate, carried, BLOCK)
    conv_out = (
        block_convolve(blocks, decay_rate, residue, entering)
        .reshape(own_chan, -1)
        .astype(jnp.bfloat16)
    )
    conv_back = lax.all_to_all(conv_out, "seq", split_axis=1, concat_axis=0, tiled=True)
    conv_back = lax.optimization_barrier(conv_back)
    gated_rows = (query_rows.astype(jnp.float32) * conv_back.astype(jnp.float32)).astype(
        jnp.bfloat16
    )
    return (gated_rows.T, new_state)


def scan_kernel(q_ref, k_ref, v_ref, rate_ref, scale_ref, residue_ref, carried_ref, gated_ref,
                state_ref, signal, ends, entering, conv):
    length, width = q_ref.shape
    modes = rate_ref.shape[0]
    chunk = length // CHUNKS
    rows_at = 256
    for lane in range(0, width, LANES):
        lanes = pl.ds(lane, LANES)

        def multiply(step, _):
            rows = pl.ds(pl.multiple_of(step * rows_at, rows_at), rows_at)
            product = k_ref[rows, lanes].astype(jnp.float32) * v_ref[rows, lanes].astype(jnp.float32)
            signal[rows, :] = product.astype(jnp.bfloat16).astype(jnp.float32)
            return 0

        lax.fori_loop(0, length // rows_at, multiply, 0)
        rates = rate_ref[:, lanes]
        residues = residue_ref[:, lanes]
        scale = scale_ref[:, lanes]
        decay = jnp.exp(-rates)
        weight = residues * scale
        chunk_decay = jnp.exp(-rates * chunk)

        def rows_of(array):
            return [jnp.broadcast_to(array[m : m + 1, :], (CHUNKS, LANES)) for m in range(modes)]

        decays = rows_of(decay)
        weights = rows_of(weight)

        def sums(step, states):
            here = signal[pl.ds(step, CHUNKS, stride=chunk), :]
            return tuple(d * s + here for d, s in zip(decays, states))

        zero = jnp.zeros((CHUNKS, LANES), jnp.float32)
        finals = lax.fori_loop(0, chunk, sums, (zero,) * modes, unroll=4)
        for m in range(modes):
            ends[m] = finals[m]
        state = carried_ref[:, lanes]
        for c in range(CHUNKS):
            entering[:, c, :] = residues * state
            state = chunk_decay * state + scale * ends[:, c, :]
        state_ref[:, lanes] = state

        def outputs(step, states):
            here = signal[pl.ds(step, CHUNKS, stride=chunk), :]
            states = tuple(d * s + w * here for d, s, w in zip(decays, states, weights))
            terms = list(states)
            while len(terms) > 1:
                terms = [a + b for a, b in zip(terms[::2], terms[1::2])] + (
                    [terms[-1]] if len(terms) % 2 else []
                )
            conv[pl.ds(step, CHUNKS, stride=chunk), :] = terms[0]
            return states

        starts = tuple(entering[m] for m in range(modes))
        lax.fori_loop(0, chunk, outputs, starts, unroll=4)

        def gate(step, _):
            rows = pl.ds(pl.multiple_of(step * rows_at, rows_at), rows_at)
            rounded = conv[rows, :].astype(jnp.bfloat16).astype(jnp.float32)
            gated_ref[rows, lanes] = (q_ref[rows, lanes].astype(jnp.float32) * rounded).astype(
                jnp.bfloat16
            )
            return 0

        lax.fori_loop(0, length // rows_at, gate, 0)


def gated_scan(rows, rate, residue, carried):
    length = rows.shape[1]
    width, modes = rate.shape
    vmem = pl.BlockSpec(memory_space=pltpu.VMEM)
    gated, state = pl.pallas_call(
        scan_kernel,
        grid=(1,),
        out_shape=(
            jax.ShapeDtypeStruct((length, width), jnp.bfloat16),
            jax.ShapeDtypeStruct((modes, width), jnp.float32),
        ),
        in_specs=[pl.BlockSpec((None, length, width), functools.partial(lambda j, i: (j, 0, 0), j)) for j in range(3)]
        + [vmem] * 4,
        out_specs=(pl.BlockSpec((length, width), lambda i: (0, 0)), vmem),
        scratch_shapes=[
            pltpu.VMEM((length, LANES), jnp.float32),
            pltpu.VMEM((modes, CHUNKS, LANES), jnp.float32),
            pltpu.VMEM((modes, CHUNKS, LANES), jnp.float32),
            pltpu.VMEM((length, LANES), jnp.float32),
        ],
        compiler_params=pltpu.CompilerParams(vmem_limit_bytes=32 * 2**20),
    )(rows, rows, rows, rate.T, mode_scale(rate).T, residue.T, carried.T)
    return gated, state.T


MESH = pl.DeviceIdType.MESH
PIECES = 2


def project_kernel(count, tokens_ref, query_ref, key_ref, value_ref, out_ref,
                   all_ref, weights_ref, fill_sem,
                  hop_send, hop_recv, side_send, side_recv, core_send, core_recv,
                  part_send, part_recv, layer_send, layer_recv):
    part, seq, chan, rep = (lax.axis_index(a) for a in ("parts", "seq", "chan", "rep"))
    rows, columns = tokens_ref.shape
    depth, outer = query_ref.shape
    width = outer // count
    half = depth // 2
    piece = rows // PIECES
    own_columns = pl.ds(pl.multiple_of(seq * width, width), width)
    matrices = (query_ref, key_ref, value_ref)

    barrier = pltpu.get_barrier_semaphore()
    mates = ({"parts": 1 - part}, {"chan": 1 - chan}, {"rep": 1 - rep})
    for mate in mates:
        pl.semaphore_signal(barrier, inc=1, device_id=mate, device_id_type=MESH)
    for step in range(1, count):
        pl.semaphore_signal(
            barrier, inc=1, device_id={"seq": lax.rem(seq + step, count)}, device_id_type=MESH
        )
    pl.semaphore_wait(barrier, count - 1 + len(mates))

    def token_block(block, side, core, p):
        top = pl.multiple_of(block * rows + p * piece, piece)
        left = pl.multiple_of((side * 2 + core) * columns, columns)
        return all_ref.at[pl.ds(top, piece), pl.ds(left, columns)]

    def own_piece(p):
        return tokens_ref.at[pl.ds(p * piece, piece), :]

    def remote(source, target, send, recv, device):
        return pltpu.make_async_remote_copy(
            src_ref=source, dst_ref=target, send_sem=send, recv_sem=recv,
            device_id=device, device_id_type=MESH,
        )

    def hop(block, p, way, source=None):
        here = token_block(block, chan, rep, p)
        device = {"seq": seq + 1 if way == 0 else seq - 1}
        return remote(here if source is None else source, here, hop_send.at[block, p, way], hop_recv.at[block, p], device)

    def side(block, p, source=None):
        here = token_block(block, chan, rep, p)
        return remote(here if source is None else source, here, side_send.at[block, p], side_recv.at[block, p], {"chan": 1 - chan})

    def side_arrival(block, p):
        there = token_block(block, 1 - chan, rep, p)
        return remote(there, there, side_send.at[block, p], side_recv.at[block, p], {"chan": 1 - chan})

    def core(block, which, p, source=None):
        here = token_block(block, chan if which == 0 else 1 - chan, rep, p)
        return remote(here if source is None else source, here, core_send.at[block, which, p], core_recv.at[block, which, p], {"rep": 1 - rep})

    def core_arrival(block, which, p):
        there = token_block(block, chan if which == 0 else 1 - chan, 1 - rep, p)
        return remote(there, there, core_send.at[block, which, p], core_recv.at[block, which, p], {"rep": 1 - rep})

    def weight_block(block, m, part_of):
        top = pl.multiple_of(block * depth + part_of * half, half)
        return weights_ref.at[m, pl.ds(top, half), :]

    def spread(target, m):
        source = matrices[m].at[
            pl.ds(pl.multiple_of(part * half, half), half),
            pl.ds(pl.multiple_of(target * width, width), width),
        ]
        return remote(source, weight_block(seq, m, part), layer_send.at[target, m], layer_recv.at[seq, m], {"seq": target})

    def spread_arrival(block, m):
        here = weight_block(block, m, part)
        return remote(here, here, layer_send.at[block, m], layer_recv.at[block, m], {"seq": block})

    def swap(block, m):
        here = weight_block(block, m, part)
        return remote(here, here, part_send.at[block, m], part_recv.at[block, m], {"parts": 1 - part})

    def swap_arrival(block, m):
        there = weight_block(block, m, 1 - part)
        return remote(there, there, part_send.at[block, m], part_recv.at[block, m], {"parts": 1 - part})

    def sources(distance):
        return ((seq >= distance, seq - distance, 0), (seq + distance < count, seq + distance, 1))

    def has_next(way):
        return seq + 1 < count if way == 0 else seq >= 1

    def send_weights(distance):
        for there, other, _ in sources(distance):
            @pl.when(there)
            def _():
                for m in range(3):
                    spread(other, m).start()

    def project(block):
        top = pl.multiple_of(block * rows, rows)

        def one(m, _):
            out_ref[m, pl.ds(top, rows), :] = jnp.dot(
                all_ref[pl.ds(top, rows), :], weights_ref[m], preferred_element_type=jnp.float32
            ).astype(jnp.bfloat16)
            return 0

        lax.fori_loop(0, 3, one, 0)

    fills = [
        pltpu.make_async_copy(
            tokens_ref,
            all_ref.at[pl.ds(pl.multiple_of(seq * rows, rows), rows),
                       pl.ds(pl.multiple_of((chan * 2 + rep) * columns, columns), columns)],
            fill_sem.at[3])
    ] + [
        pltpu.make_async_copy(
            matrices[m].at[:, own_columns],
            weights_ref.at[m, pl.ds(pl.multiple_of(seq * depth, depth), depth), :],
            fill_sem.at[m])
        for m in range(3)
    ]
    for distance in range(1, count):
        send_weights(distance)
    for p in range(PIECES):
        for way in range(2):
            @pl.when(has_next(way))
            def _():
                hop(seq, p, way, own_piece(p)).start()
        side(seq, p, own_piece(p)).start()
        core(seq, 0, p, own_piece(p)).start()
    for fill in fills:
        fill.start()

    def pass_side(block):
        for p in range(PIECES):
            side_arrival(block, p).wait_recv()
            core(block, 1, p).start()

    pass_side(seq)
    for distance in range(1, count):
        for m in range(3):
            for there, other, _ in sources(distance):
                @pl.when(there)
                def _():
                    spread_arrival(other, m).wait_recv()
                    swap(other, m).start()
    for fill in fills:
        fill.wait()

    def core_arrivals(block):
        for p in range(PIECES):
            for which in range(2):
                core_arrival(block, which, p).wait_recv()

    def finish(distance):
        if distance == 0:
            core_arrivals(seq)
            project(seq)
        else:
            for there, other, _ in sources(distance):
                @pl.when(there)
                def _():
                    pass_side(other)
                    core_arrivals(other)
                    project(other)

    for distance in range(1, count):
        for p in range(PIECES):
            for there, other, way in sources(distance):
                @pl.when(there)
                def _():
                    hop(other, p, way).wait_recv()

                    @pl.when(has_next(way))
                    def _():
                        hop(other, p, way).start()

                    side(other, p).start()
                    core(other, 0, p).start()
        if distance == 1:
            for there, other, _ in [s for d in range(1, count) for s in sources(d)]:
                @pl.when(there)
                def _():
                    for m in range(3):
                        swap_arrival(other, m).wait_recv()
        finish(distance - 1)
    finish(count - 1)

    for p in range(PIECES):
        for way in range(2):
            @pl.when(has_next(way))
            def _():
                hop(seq, p, way, own_piece(p)).wait_send()
        side(seq, p, own_piece(p)).wait_send()
        core(seq, 0, p, own_piece(p)).wait_send()
        core(seq, 1, p).wait_send()
    for distance in range(1, count):
        for there, other, way in sources(distance):
            @pl.when(there)
            def _():
                for p in range(PIECES):
                    @pl.when(has_next(way))
                    def _():
                        hop(other, p, way).wait_send()

                    side(other, p).wait_send()
                    for which in range(2):
                        core(other, which, p).wait_send()
                for m in range(3):
                    spread(other, m).wait_send()
                    swap(other, m).wait_send()


def project_all(tokens, w_query, w_key, w_value, count):
    rows, columns = tokens.shape
    depth, outer = w_query.shape
    width = outer // count
    anywhere = pl.BlockSpec(memory_space=pl.ANY)
    dma = pltpu.SemaphoreType.DMA
    return pl.pallas_call(
        functools.partial(project_kernel, count),
        out_shape=jax.ShapeDtypeStruct((3, rows * count, width), jnp.bfloat16),
        in_specs=[anywhere] * 4,
        out_specs=pl.BlockSpec(memory_space=pltpu.VMEM),
        scratch_shapes=[
            pltpu.VMEM((rows * count, columns * 4), jnp.bfloat16),
            pltpu.VMEM((3, depth * count, width), jnp.bfloat16),
            dma((4,)),
            dma((count, PIECES, 2)), dma((count, PIECES)),
            dma((count, PIECES)), dma((count, PIECES)),
            dma((count, 2, PIECES)), dma((count, 2, PIECES)),
            dma((count, 3)), dma((count, 3)),
            dma((count, 3)), dma((count, 3)),
        ],
        compiler_params=pltpu.CompilerParams(
            collective_id=0, has_side_effects=True, vmem_limit_bytes=50 * 2**20
        ),
    )(tokens, w_query, w_key, w_value)


def per_device_channels(tokens, w_query, w_key, w_value, decay_rate, residue, carried):
    count = lax.axis_size("seq")
    rows = project_all(tokens, w_query, w_key, w_value, count)
    gated, new_state = gated_scan(rows, decay_rate, residue, carried)
    gated = lax.all_to_all(gated, "seq", split_axis=0, concat_axis=1, tiled=True)
    return gated, new_state


def solution(mesh):
    in_specs = (
        P(("parts", "seq"), ("chan", "rep")),
        P("seq", ("chan", "rep")),
        P("seq", ("chan", "rep")),
        P("seq", ("chan", "rep")),
        P(("chan", "rep", "seq"), None),
        P(("chan", "rep", "seq"), None),
        P(("parts", "chan", "rep", "seq"), None),
    )
    out_specs = (P(("parts", "seq"), ("chan", "rep")), P(("parts", "chan", "rep", "seq"), None))

    def body(*arrays):
        own_channels = arrays[4].shape[0]
        mates = all(mesh.shape[a] == 2 for a in ("parts", "chan", "rep"))
        chosen = per_device_channels if own_channels % LANES == 0 and mates else per_device
        return chosen(*arrays)

    return jax.shard_map(body, mesh=mesh, in_specs=in_specs, out_specs=out_specs, check_vma=False)
```

```python
import functools

import jax
import jax.numpy as jnp
from jax import lax
from jax.experimental import pallas as pl
from jax.experimental.pallas import tpu as pltpu
from jax.sharding import PartitionSpec as P

BLOCK = 128
LANES = 128
CHUNKS = 8
MESH = pl.DeviceIdType.MESH


HIGHEST_PRECISION = lax.Precision.HIGHEST


def mode_scale(decay_rates):
    return jnp.sqrt(-jnp.expm1(-2.0 * decay_rates))


def local_ends(blocks, decay_rates):
    block_width = blocks.shape[2]
    offsets = jnp.arange(block_width, dtype=jnp.float32)
    tail_powers = jnp.exp(-decay_rates[:, :, None] * (block_width - 1.0 - offsets)[None, None, :])
    sums_here = jnp.einsum("cnb,cmb->cnm", blocks, tail_powers, precision=HIGHEST_PRECISION)
    return mode_scale(decay_rates)[:, None, :] * sums_here


def combine_states(earlier, later):
    return (earlier[0] * later[0], later[0] * earlier[1] + later[1])


def block_sums(block_ends, decay_rates, block_width):
    step_decay = jnp.broadcast_to(jnp.exp(-decay_rates * block_width)[:, None, :], block_ends.shape)
    unused_decay, running = lax.associative_scan(combine_states, (step_decay, block_ends), axis=1)
    return running


def entering_states(running, decay_rates, start_state, block_width):
    count_blocks = running.shape[1]
    block_starts = jnp.arange(count_blocks, dtype=jnp.float32) * block_width
    decayed = (
        jnp.exp(-decay_rates[:, None, :] * block_starts[None, :, None]) * start_state[:, None, :]
    )
    earlier_sums = jnp.concatenate([jnp.zeros_like(running[:, :1]), running[:, :-1]], axis=1)
    final_state = (
        jnp.exp(-decay_rates * (count_blocks * block_width)) * start_state + running[:, -1]
    )
    return (decayed + earlier_sums, final_state)


def block_convolve(blocks, decay_rates, residues, entering):
    block_width = blocks.shape[2]
    offsets = jnp.arange(block_width, dtype=jnp.float32)
    powers = jnp.exp(-decay_rates[:, :, None] * offsets[None, None, :])
    kernel = jnp.sum((residues * mode_scale(decay_rates))[:, :, None] * powers, axis=1)
    out_index = jnp.arange(block_width, dtype=jnp.int32)[:, None]
    in_index = jnp.arange(block_width, dtype=jnp.int32)[None, :]
    lag = jnp.maximum(out_index - in_index, 0)
    causal = (out_index >= in_index).astype(jnp.float32)
    toeplitz = kernel[:, lag] * causal[None, :, :]
    direct = jnp.einsum("cij,cnj->cni", toeplitz, blocks, precision=HIGHEST_PRECISION)
    leading = residues[:, :, None] * jnp.exp(
        -decay_rates[:, :, None] * (offsets + 1.0)[None, None, :]
    )
    return direct + jnp.einsum("cnm,cmb->cnb", entering, leading, precision=HIGHEST_PRECISION)


def per_device(tokens, w_query, w_key, w_value, decay_rate, residue, carried):
    gathered = lax.all_gather(tokens, ("chan", "rep"), axis=1, tiled=True)
    pieces = (
        lax.all_gather(w_query, "seq", axis=0, tiled=True),
        lax.all_gather(w_key, "seq", axis=0, tiled=True),
        lax.all_gather(w_value, "seq", axis=0, tiled=True),
    )
    query_acc, key_acc, value_acc = tuple(
        (
            lax.dot_general(
                weight_piece, gathered, (((0,), (1,)), ((), ())), preferred_element_type=jnp.float32
            )
            for weight_piece in pieces
        )
    )
    query_rows = query_acc.astype(jnp.bfloat16)
    key_rows = key_acc.astype(jnp.bfloat16)
    value_rows = value_acc.astype(jnp.bfloat16)
    query_rows, key_rows, value_rows = lax.optimization_barrier((query_rows, key_rows, value_rows))
    product = (key_rows.astype(jnp.float32) * value_rows.astype(jnp.float32)).astype(jnp.bfloat16)
    owned = lax.all_to_all(product, "seq", split_axis=0, concat_axis=1, tiled=True)
    own_chan = owned.shape[0]
    blocks = owned.astype(jnp.float32).reshape(own_chan, -1, BLOCK)
    block_end = local_ends(blocks, decay_rate)
    running = block_sums(block_end, decay_rate, BLOCK)
    entering, new_state = entering_states(running, decay_rate, carried, BLOCK)
    conv_out = (
        block_convolve(blocks, decay_rate, residue, entering)
        .reshape(own_chan, -1)
        .astype(jnp.bfloat16)
    )
    conv_back = lax.all_to_all(conv_out, "seq", split_axis=1, concat_axis=0, tiled=True)
    conv_back = lax.optimization_barrier(conv_back)
    gated_rows = (query_rows.astype(jnp.float32) * conv_back.astype(jnp.float32)).astype(
        jnp.bfloat16
    )
    return (gated_rows.T, new_state)


def scan_kernel(count, q_ref, k_ref, v_ref, rate_hbm, scale_hbm, residue_hbm, carried_hbm, out_ref,
                state_ref, rate_ref, scale_ref, residue_ref, carried_ref, signal, ends, entering, conv,
                gated_ref, fill_sem, own_sem, send_sem, recv_sem):
    seq = lax.axis_index("seq")
    barrier = pltpu.get_barrier_semaphore()
    for step in range(1, count):
        pl.semaphore_signal(
            barrier, inc=1, device_id={"seq": lax.rem(seq + step, count)}, device_id_type=MESH
        )
    fills = [
        pltpu.make_async_copy(source, target, fill_sem.at[n])
        for n, (source, target) in enumerate((
            (rate_hbm, rate_ref), (scale_hbm, scale_ref),
            (residue_hbm, residue_ref), (carried_hbm, carried_ref),
        ))
    ]
    for fill in fills:
        fill.start()
    length, width = q_ref.shape
    rows_out = length // count

    def columns_of(source, lane):
        return out_ref.at[:, pl.ds(pl.multiple_of(source * width + lane, LANES), LANES)]

    def block_of(target, lane):
        top = pl.multiple_of(target * rows_out, rows_out)
        return gated_ref.at[pl.ds(top, rows_out), pl.ds(lane, LANES)]

    def give(step, lane):
        target = lax.rem(seq + step, count)
        group = lane // LANES
        return pltpu.make_async_remote_copy(
            src_ref=block_of(target, lane), dst_ref=columns_of(seq, lane),
            send_sem=send_sem.at[target, group], recv_sem=recv_sem.at[seq, group],
            device_id={"seq": target}, device_id_type=MESH,
        )

    def take(step, lane):
        source = lax.rem(seq + step, count)
        group = lane // LANES
        return pltpu.make_async_remote_copy(
            src_ref=columns_of(source, lane), dst_ref=columns_of(source, lane),
            send_sem=send_sem.at[source, group], recv_sem=recv_sem.at[source, group],
            device_id={"seq": source}, device_id_type=MESH,
        )

    def keep(lane):
        return pltpu.make_async_copy(
            block_of(seq, lane), columns_of(seq, lane), own_sem.at[lane // LANES]
        )

    modes = rate_ref.shape[0]
    chunk = length // CHUNKS
    rows_at = 256
    for lane in range(0, width, LANES):
        lanes = pl.ds(lane, LANES)

        def multiply(step, _):
            rows = pl.ds(pl.multiple_of(step * rows_at, rows_at), rows_at)
            product = k_ref[rows, lanes].astype(jnp.float32) * v_ref[rows, lanes].astype(jnp.float32)
            signal[rows, :] = product.astype(jnp.bfloat16).astype(jnp.float32)
            return 0

        lax.fori_loop(0, length // rows_at, multiply, 0)
        if lane == 0:
            for fill in fills:
                fill.wait()
        rates = rate_ref[:, lanes]
        residues = residue_ref[:, lanes]
        scale = scale_ref[:, lanes]
        decay = jnp.exp(-rates)
        weight = residues * scale
        chunk_decay = jnp.exp(-rates * chunk)

        def rows_of(array):
            return [jnp.broadcast_to(array[m : m + 1, :], (CHUNKS, LANES)) for m in range(modes)]

        decays = rows_of(decay)
        weights = rows_of(weight)

        def sums(step, states):
            here = signal[pl.ds(step, CHUNKS, stride=chunk), :]
            return tuple(d * s + here for d, s in zip(decays, states))

        zero = jnp.zeros((CHUNKS, LANES), jnp.float32)
        finals = lax.fori_loop(0, chunk, sums, (zero,) * modes, unroll=4)
        for m in range(modes):
            ends[m] = finals[m]
        state = carried_ref[:, lanes]
        for c in range(CHUNKS):
            entering[:, c, :] = residues * state
            state = chunk_decay * state + scale * ends[:, c, :]
        state_ref[:, lanes] = state

        def outputs(step, states):
            here = signal[pl.ds(step, CHUNKS, stride=chunk), :]
            states = tuple(d * s + w * here for d, s, w in zip(decays, states, weights))
            terms = list(states)
            while len(terms) > 1:
                terms = [a + b for a, b in zip(terms[::2], terms[1::2])] + (
                    [terms[-1]] if len(terms) % 2 else []
                )
            conv[pl.ds(step, CHUNKS, stride=chunk), :] = terms[0]
            return states

        starts = tuple(entering[m] for m in range(modes))
        lax.fori_loop(0, chunk, outputs, starts, unroll=4)

        def gate(step, _):
            rows = pl.ds(pl.multiple_of(step * rows_at, rows_at), rows_at)
            rounded = conv[rows, :].astype(jnp.bfloat16).astype(jnp.float32)
            gated_ref[rows, lanes] = (q_ref[rows, lanes].astype(jnp.float32) * rounded).astype(
                jnp.bfloat16
            )
            return 0

        lax.fori_loop(0, length // rows_at, gate, 0)
        if lane == 0:
            pl.semaphore_wait(barrier, count - 1)
        for step in range(1, count):
            give(step, lane).start()
        keep(lane).start()
    for lane in range(0, width, LANES):
        keep(lane).wait()
        for step in range(1, count):
            take(step, lane).wait_recv()
            give(step, lane).wait_send()


def gated_scan(rows, rate, residue, carried, count):
    length = rows.shape[1]
    width, modes = rate.shape
    vmem = pl.BlockSpec(memory_space=pltpu.VMEM)
    anywhere = pl.BlockSpec(memory_space=pl.ANY)
    dma = pltpu.SemaphoreType.DMA
    table = pltpu.VMEM((modes, width), jnp.float32)
    gated, state = pl.pallas_call(
        functools.partial(scan_kernel, count),
        grid=(1,),
        out_shape=(
            jax.ShapeDtypeStruct((length // count, width * count), jnp.bfloat16),
            jax.ShapeDtypeStruct((modes, width), jnp.float32),
        ),
        in_specs=[pl.BlockSpec((None, length, width), functools.partial(lambda j, i: (j, 0, 0), j)) for j in range(3)]
        + [anywhere] * 4,
        out_specs=(anywhere, vmem),
        scratch_shapes=[table] * 4 + [
            pltpu.VMEM((length, LANES), jnp.float32),
            pltpu.VMEM((modes, CHUNKS, LANES), jnp.float32),
            pltpu.VMEM((modes, CHUNKS, LANES), jnp.float32),
            pltpu.VMEM((length, LANES), jnp.float32),
            pltpu.VMEM((length, width), jnp.bfloat16),
            dma((4,)), dma((width // LANES,)),
            dma((count, width // LANES)), dma((count, width // LANES)),
        ],
        compiler_params=pltpu.CompilerParams(
            collective_id=1, has_side_effects=True, vmem_limit_bytes=32 * 2**20
        ),
    )(rows, rows, rows, rate.T, mode_scale(rate).T, residue.T, carried.T)
    return gated, state.T


PIECES = 2


def project_kernel(count, tokens_ref, query_ref, key_ref, value_ref, out_ref,
                   all_ref, weights_ref, fill_sem,
                  hop_send, hop_recv, side_send, side_recv, core_send, core_recv,
                  part_send, part_recv, layer_send, layer_recv):
    part, seq, chan, rep = (lax.axis_index(a) for a in ("parts", "seq", "chan", "rep"))
    rows, columns = tokens_ref.shape
    depth, outer = query_ref.shape
    width = outer // count
    half = depth // 2
    piece = rows // PIECES
    own_columns = pl.ds(pl.multiple_of(seq * width, width), width)
    matrices = (query_ref, key_ref, value_ref)

    barrier = pltpu.get_barrier_semaphore()
    mates = ({"parts": 1 - part}, {"chan": 1 - chan}, {"rep": 1 - rep})
    for mate in mates:
        pl.semaphore_signal(barrier, inc=1, device_id=mate, device_id_type=MESH)
    for step in range(1, count):
        pl.semaphore_signal(
            barrier, inc=1, device_id={"seq": lax.rem(seq + step, count)}, device_id_type=MESH
        )
    pl.semaphore_wait(barrier, count - 1 + len(mates))

    def token_block(block, side, core, p):
        top = pl.multiple_of(block * rows + p * piece, piece)
        left = pl.multiple_of((side * 2 + core) * columns, columns)
        return all_ref.at[pl.ds(top, piece), pl.ds(left, columns)]

    def own_piece(p):
        return tokens_ref.at[pl.ds(p * piece, piece), :]

    def remote(source, target, send, recv, device):
        return pltpu.make_async_remote_copy(
            src_ref=source, dst_ref=target, send_sem=send, recv_sem=recv,
            device_id=device, device_id_type=MESH,
        )

    def hop(block, p, way, source=None):
        here = token_block(block, chan, rep, p)
        device = {"seq": seq + 1 if way == 0 else seq - 1}
        return remote(here if source is None else source, here, hop_send.at[block, p, way], hop_recv.at[block, p], device)

    def side(block, p, source=None):
        here = token_block(block, chan, rep, p)
        return remote(here if source is None else source, here, side_send.at[block, p], side_recv.at[block, p], {"chan": 1 - chan})

    def side_arrival(block, p):
        there = token_block(block, 1 - chan, rep, p)
        return remote(there, there, side_send.at[block, p], side_recv.at[block, p], {"chan": 1 - chan})

    def core(block, which, p, source=None):
        here = token_block(block, chan if which == 0 else 1 - chan, rep, p)
        return remote(here if source is None else source, here, core_send.at[block, which, p], core_recv.at[block, which, p], {"rep": 1 - rep})

    def core_arrival(block, which, p):
        there = token_block(block, chan if which == 0 else 1 - chan, 1 - rep, p)
        return remote(there, there, core_send.at[block, which, p], core_recv.at[block, which, p], {"rep": 1 - rep})

    def weight_block(block, m, part_of):
        top = pl.multiple_of(block * depth + part_of * half, half)
        return weights_ref.at[m, pl.ds(top, half), :]

    def spread(target, m):
        source = matrices[m].at[
            pl.ds(pl.multiple_of(part * half, half), half),
            pl.ds(pl.multiple_of(target * width, width), width),
        ]
        return remote(source, weight_block(seq, m, part), layer_send.at[target, m], layer_recv.at[seq, m], {"seq": target})

    def spread_arrival(block, m):
        here = weight_block(block, m, part)
        return remote(here, here, layer_send.at[block, m], layer_recv.at[block, m], {"seq": block})

    def swap(block, m):
        here = weight_block(block, m, part)
        return remote(here, here, part_send.at[block, m], part_recv.at[block, m], {"parts": 1 - part})

    def swap_arrival(block, m):
        there = weight_block(block, m, 1 - part)
        return remote(there, there, part_send.at[block, m], part_recv.at[block, m], {"parts": 1 - part})

    def sources(distance):
        return ((seq >= distance, seq - distance, 0), (seq + distance < count, seq + distance, 1))

    def has_next(way):
        return seq + 1 < count if way == 0 else seq >= 1

    def send_weights(distance):
        for there, other, _ in sources(distance):
            @pl.when(there)
            def _():
                for m in range(3):
                    spread(other, m).start()

    def project(block):
        top = pl.multiple_of(block * rows, rows)

        def one(m, _):
            out_ref[m, pl.ds(top, rows), :] = jnp.dot(
                all_ref[pl.ds(top, rows), :], weights_ref[m], preferred_element_type=jnp.float32
            ).astype(jnp.bfloat16)
            return 0

        lax.fori_loop(0, 3, one, 0)

    fills = [
        pltpu.make_async_copy(
            tokens_ref,
            all_ref.at[pl.ds(pl.multiple_of(seq * rows, rows), rows),
                       pl.ds(pl.multiple_of((chan * 2 + rep) * columns, columns), columns)],
            fill_sem.at[3])
    ] + [
        pltpu.make_async_copy(
            matrices[m].at[:, own_columns],
            weights_ref.at[m, pl.ds(pl.multiple_of(seq * depth, depth), depth), :],
            fill_sem.at[m])
        for m in range(3)
    ]
    for distance in range(1, count):
        send_weights(distance)
    for p in range(PIECES):
        for way in range(2):
            @pl.when(has_next(way))
            def _():
                hop(seq, p, way, own_piece(p)).start()
        side(seq, p, own_piece(p)).start()
        core(seq, 0, p, own_piece(p)).start()
    for fill in fills:
        fill.start()

    def pass_side(block):
        for p in range(PIECES):
            side_arrival(block, p).wait_recv()
            core(block, 1, p).start()

    pass_side(seq)
    for distance in range(1, count):
        for m in range(3):
            for there, other, _ in sources(distance):
                @pl.when(there)
                def _():
                    spread_arrival(other, m).wait_recv()
                    swap(other, m).start()
    for fill in fills:
        fill.wait()

    def core_arrivals(block):
        for p in range(PIECES):
            for which in range(2):
                core_arrival(block, which, p).wait_recv()

    def finish(distance):
        if distance == 0:
            core_arrivals(seq)
            project(seq)
        else:
            for there, other, _ in sources(distance):
                @pl.when(there)
                def _():
                    pass_side(other)
                    core_arrivals(other)
                    project(other)

    for distance in range(1, count):
        for p in range(PIECES):
            for there, other, way in sources(distance):
                @pl.when(there)
                def _():
                    hop(other, p, way).wait_recv()

                    @pl.when(has_next(way))
                    def _():
                        hop(other, p, way).start()

                    side(other, p).start()
                    core(other, 0, p).start()
        if distance == 1:
            for there, other, _ in [s for d in range(1, count) for s in sources(d)]:
                @pl.when(there)
                def _():
                    for m in range(3):
                        swap_arrival(other, m).wait_recv()
        finish(distance - 1)
    finish(count - 1)

    for p in range(PIECES):
        for way in range(2):
            @pl.when(has_next(way))
            def _():
                hop(seq, p, way, own_piece(p)).wait_send()
        side(seq, p, own_piece(p)).wait_send()
        core(seq, 0, p, own_piece(p)).wait_send()
        core(seq, 1, p).wait_send()
    for distance in range(1, count):
        for there, other, way in sources(distance):
            @pl.when(there)
            def _():
                for p in range(PIECES):
                    @pl.when(has_next(way))
                    def _():
                        hop(other, p, way).wait_send()

                    side(other, p).wait_send()
                    for which in range(2):
                        core(other, which, p).wait_send()
                for m in range(3):
                    spread(other, m).wait_send()
                    swap(other, m).wait_send()


def project_all(tokens, w_query, w_key, w_value, count):
    rows, columns = tokens.shape
    depth, outer = w_query.shape
    width = outer // count
    anywhere = pl.BlockSpec(memory_space=pl.ANY)
    dma = pltpu.SemaphoreType.DMA
    return pl.pallas_call(
        functools.partial(project_kernel, count),
        out_shape=jax.ShapeDtypeStruct((3, rows * count, width), jnp.bfloat16),
        in_specs=[anywhere] * 4,
        out_specs=pl.BlockSpec(memory_space=pltpu.VMEM),
        scratch_shapes=[
            pltpu.VMEM((rows * count, columns * 4), jnp.bfloat16),
            pltpu.VMEM((3, depth * count, width), jnp.bfloat16),
            dma((4,)),
            dma((count, PIECES, 2)), dma((count, PIECES)),
            dma((count, PIECES)), dma((count, PIECES)),
            dma((count, 2, PIECES)), dma((count, 2, PIECES)),
            dma((count, 3)), dma((count, 3)),
            dma((count, 3)), dma((count, 3)),
        ],
        compiler_params=pltpu.CompilerParams(
            collective_id=0, has_side_effects=True, vmem_limit_bytes=50 * 2**20
        ),
    )(tokens, w_query, w_key, w_value)


def per_device_channels(tokens, w_query, w_key, w_value, decay_rate, residue, carried):
    count = lax.axis_size("seq")
    rows = project_all(tokens, w_query, w_key, w_value, count)
    return gated_scan(rows, decay_rate, residue, carried, count)


def solution(mesh):
    in_specs = (
        P(("parts", "seq"), ("chan", "rep")),
        P("seq", ("chan", "rep")),
        P("seq", ("chan", "rep")),
        P("seq", ("chan", "rep")),
        P(("chan", "rep", "seq"), None),
        P(("chan", "rep", "seq"), None),
        P(("parts", "chan", "rep", "seq"), None),
    )
    out_specs = (P(("parts", "seq"), ("chan", "rep")), P(("parts", "chan", "rep", "seq"), None))

    def body(*arrays):
        own_channels = arrays[4].shape[0]
        mates = all(mesh.shape[a] == 2 for a in ("parts", "chan", "rep"))
        chosen = per_device_channels if own_channels % LANES == 0 and mates else per_device
        return chosen(*arrays)

    return jax.shard_map(body, mesh=mesh, in_specs=in_specs, out_specs=out_specs, check_vma=False)
```

```python
import functools

import jax
import jax.numpy as jnp
from jax import lax
from jax.experimental import pallas as pl
from jax.experimental.pallas import tpu as pltpu
from jax.sharding import PartitionSpec as P

BLOCK = 128
LANES = 128
CHUNKS = 8
MESH = pl.DeviceIdType.MESH


HIGHEST_PRECISION = lax.Precision.HIGHEST


def mode_scale(decay_rates):
    return jnp.sqrt(-jnp.expm1(-2.0 * decay_rates))


def local_ends(blocks, decay_rates):
    block_width = blocks.shape[2]
    offsets = jnp.arange(block_width, dtype=jnp.float32)
    tail_powers = jnp.exp(-decay_rates[:, :, None] * (block_width - 1.0 - offsets)[None, None, :])
    sums_here = jnp.einsum("cnb,cmb->cnm", blocks, tail_powers, precision=HIGHEST_PRECISION)
    return mode_scale(decay_rates)[:, None, :] * sums_here


def combine_states(earlier, later):
    return (earlier[0] * later[0], later[0] * earlier[1] + later[1])


def block_sums(block_ends, decay_rates, block_width):
    step_decay = jnp.broadcast_to(jnp.exp(-decay_rates * block_width)[:, None, :], block_ends.shape)
    unused_decay, running = lax.associative_scan(combine_states, (step_decay, block_ends), axis=1)
    return running


def entering_states(running, decay_rates, start_state, block_width):
    count_blocks = running.shape[1]
    block_starts = jnp.arange(count_blocks, dtype=jnp.float32) * block_width
    decayed = (
        jnp.exp(-decay_rates[:, None, :] * block_starts[None, :, None]) * start_state[:, None, :]
    )
    earlier_sums = jnp.concatenate([jnp.zeros_like(running[:, :1]), running[:, :-1]], axis=1)
    final_state = (
        jnp.exp(-decay_rates * (count_blocks * block_width)) * start_state + running[:, -1]
    )
    return (decayed + earlier_sums, final_state)


def block_convolve(blocks, decay_rates, residues, entering):
    block_width = blocks.shape[2]
    offsets = jnp.arange(block_width, dtype=jnp.float32)
    powers = jnp.exp(-decay_rates[:, :, None] * offsets[None, None, :])
    kernel = jnp.sum((residues * mode_scale(decay_rates))[:, :, None] * powers, axis=1)
    out_index = jnp.arange(block_width, dtype=jnp.int32)[:, None]
    in_index = jnp.arange(block_width, dtype=jnp.int32)[None, :]
    lag = jnp.maximum(out_index - in_index, 0)
    causal = (out_index >= in_index).astype(jnp.float32)
    toeplitz = kernel[:, lag] * causal[None, :, :]
    direct = jnp.einsum("cij,cnj->cni", toeplitz, blocks, precision=HIGHEST_PRECISION)
    leading = residues[:, :, None] * jnp.exp(
        -decay_rates[:, :, None] * (offsets + 1.0)[None, None, :]
    )
    return direct + jnp.einsum("cnm,cmb->cnb", entering, leading, precision=HIGHEST_PRECISION)


def per_device(tokens, w_query, w_key, w_value, decay_rate, residue, carried):
    gathered = lax.all_gather(tokens, ("chan", "rep"), axis=1, tiled=True)
    pieces = (
        lax.all_gather(w_query, "seq", axis=0, tiled=True),
        lax.all_gather(w_key, "seq", axis=0, tiled=True),
        lax.all_gather(w_value, "seq", axis=0, tiled=True),
    )
    query_acc, key_acc, value_acc = tuple(
        (
            lax.dot_general(
                weight_piece, gathered, (((0,), (1,)), ((), ())), preferred_element_type=jnp.float32
            )
            for weight_piece in pieces
        )
    )
    query_rows = query_acc.astype(jnp.bfloat16)
    key_rows = key_acc.astype(jnp.bfloat16)
    value_rows = value_acc.astype(jnp.bfloat16)
    query_rows, key_rows, value_rows = lax.optimization_barrier((query_rows, key_rows, value_rows))
    product = (key_rows.astype(jnp.float32) * value_rows.astype(jnp.float32)).astype(jnp.bfloat16)
    owned = lax.all_to_all(product, "seq", split_axis=0, concat_axis=1, tiled=True)
    own_chan = owned.shape[0]
    blocks = owned.astype(jnp.float32).reshape(own_chan, -1, BLOCK)
    block_end = local_ends(blocks, decay_rate)
    running = block_sums(block_end, decay_rate, BLOCK)
    entering, new_state = entering_states(running, decay_rate, carried, BLOCK)
    conv_out = (
        block_convolve(blocks, decay_rate, residue, entering)
        .reshape(own_chan, -1)
        .astype(jnp.bfloat16)
    )
    conv_back = lax.all_to_all(conv_out, "seq", split_axis=1, concat_axis=0, tiled=True)
    conv_back = lax.optimization_barrier(conv_back)
    gated_rows = (query_rows.astype(jnp.float32) * conv_back.astype(jnp.float32)).astype(
        jnp.bfloat16
    )
    return (gated_rows.T, new_state)


def scan_kernel(count, q_ref, k_ref, v_ref, rate_hbm, scale_hbm, residue_hbm, carried_hbm, out_ref,
                state_ref, rate_ref, scale_ref, residue_ref, carried_ref, signal, ends, entering, conv,
                gated_ref, fill_sem, own_sem, send_sem, recv_sem):
    seq = lax.axis_index("seq")
    barrier = pltpu.get_barrier_semaphore()
    for step in range(1, count):
        pl.semaphore_signal(
            barrier, inc=1, device_id={"seq": lax.rem(seq + step, count)}, device_id_type=MESH
        )
    fills = [
        pltpu.make_async_copy(source, target, fill_sem.at[n])
        for n, (source, target) in enumerate((
            (rate_hbm, rate_ref), (scale_hbm, scale_ref),
            (residue_hbm, residue_ref), (carried_hbm, carried_ref),
        ))
    ]
    for fill in fills:
        fill.start()
    length, width = q_ref.shape
    rows_out = length // count

    def columns_of(source, lane):
        return out_ref.at[:, pl.ds(pl.multiple_of(source * width + lane, LANES), LANES)]

    def block_of(target, lane):
        top = pl.multiple_of(target * rows_out, rows_out)
        return gated_ref.at[pl.ds(top, rows_out), pl.ds(lane, LANES)]

    def give(step, lane):
        target = lax.rem(seq + step, count)
        group = lane // LANES
        return pltpu.make_async_remote_copy(
            src_ref=block_of(target, lane), dst_ref=columns_of(seq, lane),
            send_sem=send_sem.at[target, group], recv_sem=recv_sem.at[seq, group],
            device_id={"seq": target}, device_id_type=MESH,
        )

    def take(step, lane):
        source = lax.rem(seq + step, count)
        group = lane // LANES
        return pltpu.make_async_remote_copy(
            src_ref=columns_of(source, lane), dst_ref=columns_of(source, lane),
            send_sem=send_sem.at[source, group], recv_sem=recv_sem.at[source, group],
            device_id={"seq": source}, device_id_type=MESH,
        )

    def keep(lane):
        return pltpu.make_async_copy(
            block_of(seq, lane), columns_of(seq, lane), own_sem.at[lane // LANES]
        )

    modes = rate_ref.shape[0]
    chunk = length // CHUNKS
    rows_at = 256
    for lane in range(0, width, LANES):
        lanes = pl.ds(lane, LANES)

        def multiply(step, _):
            rows = pl.ds(pl.multiple_of(step * rows_at, rows_at), rows_at)
            product = k_ref[rows, lanes].astype(jnp.float32) * v_ref[rows, lanes].astype(jnp.float32)
            signal[rows, :] = product.astype(jnp.bfloat16).astype(jnp.float32)
            return 0

        lax.fori_loop(0, length // rows_at, multiply, 0)
        if lane == 0:
            for fill in fills:
                fill.wait()
        rates = rate_ref[:, lanes]
        residues = residue_ref[:, lanes]
        scale = scale_ref[:, lanes]
        decay = jnp.exp(-rates)
        weight = residues * scale
        chunk_decay = jnp.exp(-rates * chunk)

        def rows_of(array):
            return [jnp.broadcast_to(array[m : m + 1, :], (CHUNKS, LANES)) for m in range(modes)]

        decays = rows_of(decay)
        weights = rows_of(weight)

        def sums(step, states):
            here = signal[pl.ds(step, CHUNKS, stride=chunk), :]
            return tuple(d * s + here for d, s in zip(decays, states))

        zero = jnp.zeros((CHUNKS, LANES), jnp.float32)
        finals = lax.fori_loop(0, chunk, sums, (zero,) * modes, unroll=4)
        for m in range(modes):
            ends[m] = finals[m]
        state = carried_ref[:, lanes]
        for c in range(CHUNKS):
            entering[:, c, :] = residues * state
            state = chunk_decay * state + scale * ends[:, c, :]
        state_ref[:, lanes] = state

        def outputs(step, states):
            here = signal[pl.ds(step, CHUNKS, stride=chunk), :]
            states = tuple(d * s + w * here for d, s, w in zip(decays, states, weights))
            terms = list(states)
            while len(terms) > 1:
                terms = [a + b for a, b in zip(terms[::2], terms[1::2])] + (
                    [terms[-1]] if len(terms) % 2 else []
                )
            conv[pl.ds(step, CHUNKS, stride=chunk), :] = terms[0]
            return states

        starts = tuple(entering[m] for m in range(modes))
        lax.fori_loop(0, chunk, outputs, starts, unroll=4)

        def gate(step, _):
            rows = pl.ds(pl.multiple_of(step * rows_at, rows_at), rows_at)
            rounded = conv[rows, :].astype(jnp.bfloat16).astype(jnp.float32)
            gated_ref[rows, lanes] = (q_ref[rows, lanes].astype(jnp.float32) * rounded).astype(
                jnp.bfloat16
            )
            return 0

        lax.fori_loop(0, length // rows_at, gate, 0)
        if lane == 0:
            pl.semaphore_wait(barrier, count - 1)
        for step in range(1, count):
            give(step, lane).start()
        keep(lane).start()
    for lane in range(0, width, LANES):
        keep(lane).wait()
        for step in range(1, count):
            take(step, lane).wait_recv()
            give(step, lane).wait_send()


def gated_scan(rows, rate, residue, carried, count):
    length = rows.shape[1]
    width, modes = rate.shape
    vmem = pl.BlockSpec(memory_space=pltpu.VMEM)
    anywhere = pl.BlockSpec(memory_space=pl.ANY)
    dma = pltpu.SemaphoreType.DMA
    table = pltpu.VMEM((modes, width), jnp.float32)
    gated, state = pl.pallas_call(
        functools.partial(scan_kernel, count),
        grid=(1,),
        out_shape=(
            jax.ShapeDtypeStruct((length // count, width * count), jnp.bfloat16),
            jax.ShapeDtypeStruct((modes, width), jnp.float32),
        ),
        in_specs=[pl.BlockSpec((None, length, width), functools.partial(lambda j, i: (j, 0, 0), j)) for j in range(3)]
        + [anywhere] * 4,
        out_specs=(anywhere, vmem),
        scratch_shapes=[table] * 4 + [
            pltpu.VMEM((length, LANES), jnp.float32),
            pltpu.VMEM((modes, CHUNKS, LANES), jnp.float32),
            pltpu.VMEM((modes, CHUNKS, LANES), jnp.float32),
            pltpu.VMEM((length, LANES), jnp.float32),
            pltpu.VMEM((length, width), jnp.bfloat16),
            dma((4,)), dma((width // LANES,)),
            dma((count, width // LANES)), dma((count, width // LANES)),
        ],
        compiler_params=pltpu.CompilerParams(
            collective_id=1, has_side_effects=True, vmem_limit_bytes=60 * 2**20
        ),
    )(rows, rows, rows, rate.T, mode_scale(rate).T, residue.T, carried.T)
    return gated, state.T


PIECES = 4


def project_kernel(count, tokens_ref, query_ref, key_ref, value_ref, out_ref,
                   all_ref, weights_ref, fill_sem,
                  hop_send, hop_recv, side_send, side_recv, core_send, core_recv,
                  part_send, part_recv, layer_send, layer_recv):
    part, seq, chan, rep = (lax.axis_index(a) for a in ("parts", "seq", "chan", "rep"))
    rows, columns = tokens_ref.shape
    depth, outer = query_ref.shape
    width = outer // count
    half = depth // 2
    piece = rows // PIECES
    own_columns = pl.ds(pl.multiple_of(seq * width, width), width)
    matrices = (query_ref, key_ref, value_ref)

    barrier = pltpu.get_barrier_semaphore()
    mates = ({"parts": 1 - part}, {"chan": 1 - chan}, {"rep": 1 - rep})
    for mate in mates:
        pl.semaphore_signal(barrier, inc=1, device_id=mate, device_id_type=MESH)
    for step in range(1, count):
        pl.semaphore_signal(
            barrier, inc=1, device_id={"seq": lax.rem(seq + step, count)}, device_id_type=MESH
        )
    pl.semaphore_wait(barrier, count - 1 + len(mates))

    def token_block(block, side, core, p):
        top = pl.multiple_of(block * rows + p * piece, piece)
        left = pl.multiple_of((side * 2 + core) * columns, columns)
        return all_ref.at[pl.ds(top, piece), pl.ds(left, columns)]

    def own_piece(p):
        return tokens_ref.at[pl.ds(p * piece, piece), :]

    def remote(source, target, send, recv, device):
        return pltpu.make_async_remote_copy(
            src_ref=source, dst_ref=target, send_sem=send, recv_sem=recv,
            device_id=device, device_id_type=MESH,
        )

    def hop(block, p, way, source=None):
        here = token_block(block, chan, rep, p)
        device = {"seq": seq + way}
        return remote(here if source is None else source, here, hop_send.at[block, p, (1 - way) // 2], hop_recv.at[block, p], device)

    def side(block, p, source=None):
        here = token_block(block, chan, rep, p)
        return remote(here if source is None else source, here, side_send.at[block, p], side_recv.at[block, p], {"chan": 1 - chan})

    def side_arrival(block, p):
        there = token_block(block, 1 - chan, rep, p)
        return remote(there, there, side_send.at[block, p], side_recv.at[block, p], {"chan": 1 - chan})

    def core(block, which, p, source=None):
        here = token_block(block, chan if which == 0 else 1 - chan, rep, p)
        return remote(here if source is None else source, here, core_send.at[block, which, p], core_recv.at[block, which, p], {"rep": 1 - rep})

    def core_arrival(block, which, p):
        there = token_block(block, chan if which == 0 else 1 - chan, 1 - rep, p)
        return remote(there, there, core_send.at[block, which, p], core_recv.at[block, which, p], {"rep": 1 - rep})

    def weight_block(block, m, part_of):
        top = pl.multiple_of(block * depth + part_of * half, half)
        return weights_ref.at[m, pl.ds(top, half), :]

    def spread(target, m):
        source = matrices[m].at[
            pl.ds(pl.multiple_of(part * half, half), half),
            pl.ds(pl.multiple_of(target * width, width), width),
        ]
        return remote(source, weight_block(seq, m, part), layer_send.at[target, m], layer_recv.at[seq, m], {"seq": target})

    def spread_arrival(block, m):
        here = weight_block(block, m, part)
        return remote(here, here, layer_send.at[block, m], layer_recv.at[block, m], {"seq": block})

    def swap(block, m):
        here = weight_block(block, m, part)
        return remote(here, here, part_send.at[block, m], part_recv.at[block, m], {"parts": 1 - part})

    def swap_arrival(block, m):
        there = weight_block(block, m, 1 - part)
        return remote(there, there, part_send.at[block, m], part_recv.at[block, m], {"parts": 1 - part})

    inward = 1 - 2 * ((2 * seq) // count)

    def inside(other):
        return (other >= 0) & (other < count)

    def sources(distance):
        near, far = seq - inward * distance, seq + inward * distance
        return ((inside(near), near, inward), (inside(far), far, -inward))

    def has_next(way):
        return inside(seq + way)

    def send_weights(distance):
        for there, other, _ in sources(distance):
            @pl.when(there)
            def _():
                for m in range(3):
                    spread(other, m).start()

    def project(block):
        top = pl.multiple_of(block * rows, rows)

        def one(m, _):
            out_ref[m, pl.ds(top, rows), :] = jnp.dot(
                all_ref[pl.ds(top, rows), :], weights_ref[m], preferred_element_type=jnp.float32
            ).astype(jnp.bfloat16)
            return 0

        lax.fori_loop(0, 3, one, 0)

    fills = [
        pltpu.make_async_copy(
            tokens_ref,
            all_ref.at[pl.ds(pl.multiple_of(seq * rows, rows), rows),
                       pl.ds(pl.multiple_of((chan * 2 + rep) * columns, columns), columns)],
            fill_sem.at[3])
    ] + [
        pltpu.make_async_copy(
            matrices[m].at[:, own_columns],
            weights_ref.at[m, pl.ds(pl.multiple_of(seq * depth, depth), depth), :],
            fill_sem.at[m])
        for m in range(3)
    ]
    for distance in range(1, count):
        send_weights(distance)
    for p in range(PIECES):
        for way in (1, -1):
            @pl.when(has_next(way))
            def _():
                hop(seq, p, way, own_piece(p)).start()
        side(seq, p, own_piece(p)).start()
        core(seq, 0, p, own_piece(p)).start()
    for fill in fills:
        fill.start()

    def pass_side(block):
        for p in range(PIECES):
            side_arrival(block, p).wait_recv()
            core(block, 1, p).start()

    pass_side(seq)
    for distance in range(1, count):
        for m in range(3):
            for there, other, _ in sources(distance):
                @pl.when(there)
                def _():
                    spread_arrival(other, m).wait_recv()
                    swap(other, m).start()
    for fill in fills:
        fill.wait()

    def core_arrivals(block):
        for p in range(PIECES):
            for which in range(2):
                core_arrival(block, which, p).wait_recv()

    def finish(distance):
        if distance == 0:
            core_arrivals(seq)
            project(seq)
        else:
            for there, other, _ in sources(distance):
                @pl.when(there)
                def _():
                    pass_side(other)
                    core_arrivals(other)
                    project(other)

    for distance in range(1, count):
        for there, other, way in sources(distance):
            for p in range(PIECES):
                @pl.when(there)
                def _():
                    hop(other, p, way).wait_recv()

                    @pl.when(has_next(way))
                    def _():
                        hop(other, p, way).start()

                    side(other, p).start()
                    core(other, 0, p).start()
        if distance == 1:
            for there, other, _ in [s for d in range(1, count) for s in sources(d)]:
                @pl.when(there)
                def _():
                    for m in range(3):
                        swap_arrival(other, m).wait_recv()
        finish(distance - 1)
    finish(count - 1)

    for p in range(PIECES):
        for way in (1, -1):
            @pl.when(has_next(way))
            def _():
                hop(seq, p, way, own_piece(p)).wait_send()
        side(seq, p, own_piece(p)).wait_send()
        core(seq, 0, p, own_piece(p)).wait_send()
        core(seq, 1, p).wait_send()
    for distance in range(1, count):
        for there, other, way in sources(distance):
            @pl.when(there)
            def _():
                for p in range(PIECES):
                    @pl.when(has_next(way))
                    def _():
                        hop(other, p, way).wait_send()

                    side(other, p).wait_send()
                    for which in range(2):
                        core(other, which, p).wait_send()
                for m in range(3):
                    spread(other, m).wait_send()
                    swap(other, m).wait_send()


def project_all(tokens, w_query, w_key, w_value, count):
    rows, columns = tokens.shape
    depth, outer = w_query.shape
    width = outer // count
    anywhere = pl.BlockSpec(memory_space=pl.ANY)
    dma = pltpu.SemaphoreType.DMA
    return pl.pallas_call(
        functools.partial(project_kernel, count),
        out_shape=jax.ShapeDtypeStruct((3, rows * count, width), jnp.bfloat16),
        in_specs=[anywhere] * 4,
        out_specs=pl.BlockSpec(memory_space=pltpu.VMEM),
        scratch_shapes=[
            pltpu.VMEM((rows * count, columns * 4), jnp.bfloat16),
            pltpu.VMEM((3, depth * count, width), jnp.bfloat16),
            dma((4,)),
            dma((count, PIECES, 2)), dma((count, PIECES)),
            dma((count, PIECES)), dma((count, PIECES)),
            dma((count, 2, PIECES)), dma((count, 2, PIECES)),
            dma((count, 3)), dma((count, 3)),
            dma((count, 3)), dma((count, 3)),
        ],
        compiler_params=pltpu.CompilerParams(
            collective_id=0, has_side_effects=True, vmem_limit_bytes=63 * 2**20
        ),
    )(tokens, w_query, w_key, w_value)


def per_device_channels(tokens, w_query, w_key, w_value, decay_rate, residue, carried):
    count = lax.axis_size("seq")
    rows = project_all(tokens, w_query, w_key, w_value, count)
    return gated_scan(rows, decay_rate, residue, carried, count)


def solution(mesh):
    in_specs = (
        P(("parts", "seq"), ("chan", "rep")),
        P("seq", ("chan", "rep")),
        P("seq", ("chan", "rep")),
        P("seq", ("chan", "rep")),
        P(("chan", "rep", "seq"), None),
        P(("chan", "rep", "seq"), None),
        P(("parts", "chan", "rep", "seq"), None),
    )
    out_specs = (P(("parts", "seq"), ("chan", "rep")), P(("parts", "chan", "rep", "seq"), None))

    def body(*arrays):
        own_channels = arrays[4].shape[0]
        mates = all(mesh.shape[a] == 2 for a in ("parts", "chan", "rep"))
        chosen = per_device_channels if own_channels % LANES == 0 and mates else per_device
        return chosen(*arrays)

    return jax.shard_map(body, mesh=mesh, in_specs=in_specs, out_specs=out_specs, check_vma=False)
```
